512 devices in a mesh: section: 8 (over z_lo), dp: 64 (over x, y, z_hi, core).
Axes of the slice: x: 4, y: 4, z: 16 (z_hi: 2, z_lo: 8; z = z_hi * 8 + z_lo), core: 2. Of those that a mesh axis runs over, the one named last changes fastest.
Arguments:
- section_input: bfloat16 [8, 256, 128, 512], P('section', 'dp'), may hold values from -6 to 6
- top_grad: bfloat16 [256, 128, 512], P('dp'), may hold values from -6 to 6
- conv_weight: bfloat16 [8, 3, 512, 512], P('section'), may hold values from -0.15625 to 0.15625
- step_table: bfloat16 [8, 50, 512], P('section'), may hold values from -4 to 4
- timesteps: int32 [256], P('dp'), may hold values from 0 to 49
- dilations: int32 [8], P('section'), may hold values from 1 to 32, as said below
Outputs:
- input_grad: bfloat16 [8, 256, 128, 512], P('section', 'dp')
- weight_grad: bfloat16 [8, 3, 512, 512], P('section')
- table_grad: bfloat16 [8, 50, 512], P('section')
The draws below stay inside these ranges and needn't reach their ends.
Inputs may be any that keep to these rules, and one draw needn't show every extreme that they name: `dilations`: each is a power of two; some section has dilation 32 and some other section dilation 1.
All inputs are finite; a program needn't handle non-finite values.
Results may differ from the reference program's by a relative error of at most 0.014.
Values may be sent and summed in bfloat16 or wider, within the bound.
A program may use at most 64 MiB of HBM per device.

```python
import math
import jax
import jax.numpy as jnp
from jax import lax

C = 512
NSTEPS = 50
SEQ = 128
DMAX = 32
BATCH = 256
N_SECTION = 8


def draw_dilations(key, part):
    first_key, second_key = jax.random.split(key)
    log_top = DMAX.bit_length() - 1
    powers = jax.random.randint(first_key, (N_SECTION,), 0, log_top + 1)
    values = jnp.power(2, powers).astype(jnp.int32)
    top_pos = jax.random.randint(second_key, (), 0, N_SECTION)
    positions = jnp.arange(N_SECTION, dtype=jnp.int32)
    values = jnp.where(positions == top_pos, DMAX, values)
    values = jnp.where(positions == (top_pos + 1) % N_SECTION, 1, values)
    return values.astype(jnp.int32)


def with_ends(values, rng, smallest, largest):
    longest = values.shape.index(max(values.shape))
    spots = []
    for shift in (0, 1):
        where = [jax.random.randint(jax.random.fold_in(rng, axis), (), 0, length) for axis, length in enumerate(values.shape)]
        where[longest] = (where[longest] + shift) % values.shape[longest]
        spots.append(tuple(where))
    return values.at[spots[0]].set(smallest).at[spots[1]].set(largest)


def level_of(key, extent, cuts, least, largest):
    def one(position, parts):
        draws = jax.random.uniform(jax.random.fold_in(jax.random.fold_in(key, 6), position), (parts,), jnp.float32, least / len(cuts), largest / len(cuts))
        return jnp.repeat(jnp.exp(draws), extent[position] // parts).reshape((-1,) + (1,) * (len(extent) - position - 1))

    factor_of = one(*cuts[0])
    for cut in cuts[1:]:
        factor_of = factor_of * one(*cut)
    return factor_of


def gaussian(stream_key, dims, scale, reach, shards=(), held_as=jnp.bfloat16):
    result = jax.random.normal(stream_key, dims, jnp.float32) * scale
    if len(shards) > 0:
        result = level_of(stream_key, dims, shards, -0.22, 0.18) * result
    return jnp.clip(result, min=-reach, max=reach).astype(held_as)


def setup_inputs(seed: int = 0) -> dict:
    splits = jax.random.split(jax.random.key(seed), 7)
    section_input = gaussian(splits[0], (N_SECTION, BATCH, SEQ, C), 1.0, 6.0, ((0, 8), (1, 64)))
    top_grad = gaussian(splits[1], (BATCH, SEQ, C), 1.0, 6.0, ((0, 64),))
    conv_weight = gaussian(splits[2], (N_SECTION, 3, C, C), (3 * C) ** -0.5, 0.15625, ((0, 8),))
    step_table = gaussian(splits[3], (N_SECTION, NSTEPS, C), 0.7, 4.0, ((0, 8),))
    timesteps = with_ends(jax.random.randint(splits[4], (BATCH,), 0, NSTEPS), jax.random.fold_in(splits[4], 1), 0, NSTEPS - 1).astype(jnp.int32)
    dilations = draw_dilations(jax.random.fold_in(splits[6], 71), 0)
    return {"section_input": section_input, "top_grad": top_grad, "conv_weight": conv_weight, "step_table": step_table, "timesteps": timesteps, "dilations": dilations}


def spread_taps(seq_rows, dilation, orientation):
    bins_count = seq_rows.shape[1]
    padded = jnp.pad(seq_rows, ((0, 0), (DMAX, DMAX), (0, 0)))
    pieces = []
    for tap_num in range(3):
        start = (DMAX + orientation * (tap_num - 1) * dilation).astype(jnp.int32)
        pieces.append(lax.dynamic_slice_in_dim(padded, start, bins_count, 1))
    return jnp.concatenate(pieces, axis=2)

def reference(section_input, top_grad, conv_weight, step_table, timesteps, dilations):
    grad_scale = 1.0 / math.sqrt(BATCH * SEQ)
    onehot = timesteps[:, None] == jnp.arange(NSTEPS, dtype=jnp.int32)[None, :]
    onehot_float = onehot.astype(jnp.float32)
    grad_now = top_grad
    input_list, weight_list, table_list = ([], [], [])
    for section_num in range(N_SECTION - 1, -1, -1):
        conv_kernel = conv_weight[section_num]
        dilation = dilations[section_num]
        step_embed = jnp.dot(onehot.astype(jnp.bfloat16), step_table[section_num], preferred_element_type=jnp.float32)
        mixed_rows = (section_input[section_num].astype(jnp.float32) + step_embed[:, None, :]).astype(jnp.bfloat16)
        fwd_taps = spread_taps(mixed_rows, dilation, 1).reshape(BATCH * SEQ, 3 * C)
        preact = jnp.dot(fwd_taps, conv_kernel.reshape(3 * C, C), preferred_element_type=jnp.float32)
        gate_value = jax.nn.sigmoid(preact)
        upstream = grad_now.reshape(BATCH * SEQ, C).astype(jnp.float32)
        grad_pre = (upstream * gate_value * (1.0 + preact * (1.0 - gate_value))).astype(jnp.bfloat16)
        back_taps = spread_taps(grad_pre.reshape(BATCH, SEQ, C), dilation, -1).reshape(BATCH * SEQ, 3 * C)
        kernel_back = jnp.transpose(conv_kernel, (0, 2, 1)).reshape(3 * C, C)
        grad_mixed = jnp.dot(back_taps, kernel_back, preferred_element_type=jnp.float32)
        grad_now = (upstream + grad_mixed).astype(jnp.bfloat16).reshape(BATCH, SEQ, C)
        weight_total = lax.dot_general(fwd_taps, grad_pre, (((0,), (0,)), ((), ())), preferred_element_type=jnp.float32)
        group_sums = lax.optimization_barrier(jnp.sum(grad_mixed.reshape(BATCH, SEQ, C), axis=1))
        table_total = jnp.dot(onehot_float.T, group_sums, precision=lax.Precision.HIGHEST)
        input_list.append(grad_now)
        weight_list.append((weight_total * grad_scale).astype(jnp.bfloat16).reshape(3, C, C))
        table_list.append((table_total * grad_scale).astype(jnp.bfloat16))
    return (jnp.stack(input_list[::-1]), jnp.stack(weight_list[::-1]), jnp.stack(table_list[::-1]))
```

```python
import functools
import math

import jax
import jax.numpy as jnp
from jax import lax
from jax.experimental import pallas as pl
from jax.experimental.pallas import tpu as pltpu
from jax.sharding import PartitionSpec as P

MESH = pl.DeviceIdType.MESH
NX, NY, NZ = 4, 4, 2
TABLE_ROWS = 64
PAD_ROWS = 128
F32 = jnp.float32
BF16 = jnp.bfloat16


def chain_kernel(
    x_ref, top_ref, w_ref, tab_ref, ts_ref, dil_ref, gout_ref, part_ref,
    wt, ht, fw, sp, bt, ups, downs, recv, tacc, top_sem, send_sem, recv_sem,
):
    sec = lax.axis_index("section")
    last = lax.axis_size("section") - 1
    groups, bins, chans = x_ref.shape
    steps = tab_ref.shape[0]
    dil = dil_ref[0]

    barrier = pltpu.get_barrier_semaphore()

    @pl.when(sec > 0)
    def _():
        pl.semaphore_signal(barrier, inc=1, device_id={"section": sec - 1}, device_id_type=MESH)

    @pl.when(sec < last)
    def _():
        pl.semaphore_signal(barrier, inc=1, device_id={"section": sec + 1}, device_id_type=MESH)

    top_copy = pltpu.make_async_copy(top_ref, recv, top_sem)

    @pl.when(sec == last)
    def _():
        top_copy.start()

    to_bin = lax.broadcasted_iota(jnp.int32, (bins, bins), 0)
    from_bin = lax.broadcasted_iota(jnp.int32, (bins, bins), 1)
    downs[...] = jnp.where(from_bin == to_bin - dil, 1.0, 0.0).astype(BF16)
    ups[...] = jnp.where(from_bin == to_bin + dil, 1.0, 0.0).astype(BF16)
    step_rows = lax.broadcasted_iota(jnp.int32, (steps, chans), 0)

    def mix(b, carry):
        row = pl.multiple_of(b * bins, bins)
        table = tab_ref[...].astype(F32)
        embed = jnp.sum(jnp.where(step_rows == ts_ref[b], table, 0.0), axis=0, keepdims=True)
        mixed = (x_ref[b].astype(F32) + embed).astype(BF16)
        fw[pl.ds(row, bins), chans : 2 * chans] = mixed
        fw[pl.ds(row, bins), 0:chans] = jnp.dot(
            downs[...], mixed, preferred_element_type=F32
        ).astype(BF16)
        fw[pl.ds(row, bins), 2 * chans :] = jnp.dot(
            ups[...], mixed, preferred_element_type=F32
        ).astype(BF16)
        return carry

    lax.fori_loop(0, groups, mix, 0)
    for c in range(0, chans, 256):
        preact = jnp.dot(fw[...], w_ref[:, c : c + 256], preferred_element_type=F32)
        gate = jax.nn.sigmoid(preact)
        sp[:, c : c + 256] = gate * (1.0 + preact * (1.0 - gate))
    for tap in range(3):
        wt[tap * chans : (tap + 1) * chans, :] = w_ref[tap * chans : (tap + 1) * chans, :].T
    tacc[...] = jnp.zeros_like(tacc)

    @pl.when(sec < last)
    def _():
        ht[...] = fw[:, chans : 2 * chans].T

    @pl.when(jnp.logical_and(sec > 0, sec < last))
    def _():
        pl.semaphore_wait(barrier, 2)

    @pl.when(jnp.logical_or(sec == 0, sec == last))
    def _():
        pl.semaphore_wait(barrier, 1)

    @pl.when(sec == last)
    def _():
        top_copy.wait()

    table_rows = lax.broadcasted_iota(jnp.int32, (TABLE_ROWS, chans), 0)

    def hop(b):
        return pltpu.make_async_remote_copy(
            src_ref=gout_ref.at[b],
            dst_ref=recv.at[b],
            send_sem=send_sem.at[b],
            recv_sem=recv_sem.at[b],
            device_id={"section": sec - 1},
            device_id_type=MESH,
        )

    def layer(b, carry):
        row = pl.multiple_of(b * bins, bins)

        @pl.when(sec < last)
        def _():
            hop(b).wait_recv()

        delta = (recv[b].astype(F32) * sp[pl.ds(row, bins), :]).astype(BF16)
        bt[pl.ds(row, bins), chans : 2 * chans] = delta
        bt[pl.ds(row, bins), 0:chans] = jnp.dot(
            ups[...], delta, preferred_element_type=F32
        ).astype(BF16)
        bt[pl.ds(row, bins), 2 * chans :] = jnp.dot(
            downs[...], delta, preferred_element_type=F32
        ).astype(BF16)
        grad = jnp.dot(bt[pl.ds(row, bins), :], wt[...], preferred_element_type=F32)
        gout_ref[b] = (recv[b].astype(F32) + grad).astype(BF16)

        @pl.when(sec > 0)
        def _():
            hop(b).start()

        total = jnp.sum(grad, axis=0, keepdims=True)
        tacc[...] += jnp.where(table_rows == ts_ref[b], total, 0.0)
        return carry

    lax.fori_loop(0, groups, layer, 0)

    @pl.when(sec == last)
    def _():
        ht[...] = fw[:, chans : 2 * chans].T

    rows = 3 * chans
    for tap in range(3):
        span = slice(tap * chans, (tap + 1) * chans)
        part_ref[span, :] = jnp.dot(ht[...], bt[:, span], preferred_element_type=F32).astype(BF16)
    part_ref[rows : rows + TABLE_ROWS, :] = tacc[...].astype(BF16)
    part_ref[rows + TABLE_ROWS :, :] = jnp.zeros((PAD_ROWS - TABLE_ROWS, chans), BF16)

    @pl.when(sec > 0)
    def _():
        for b in range(groups):
            hop(b).wait_send()


def chain(saved, top, weight, table, timesteps, dilations):
    groups, bins, chans = saved.shape
    vmem = pl.BlockSpec(memory_space=pltpu.VMEM)
    smem = pl.BlockSpec(memory_space=pltpu.SMEM)
    rows = 3 * chans
    return pl.pallas_call(
        chain_kernel,
        out_shape=(
            jax.ShapeDtypeStruct((groups, bins, chans), BF16),
            jax.ShapeDtypeStruct((rows + PAD_ROWS, chans), BF16),
        ),
        in_specs=[vmem, pl.BlockSpec(memory_space=pl.ANY), vmem, vmem, smem, smem],
        out_specs=(vmem, vmem),
        scratch_shapes=[
            pltpu.VMEM((rows, chans), BF16),
            pltpu.VMEM((chans, groups * bins), BF16),
            pltpu.VMEM((groups * bins, rows), BF16),
            pltpu.VMEM((groups * bins, chans), F32),
            pltpu.VMEM((groups * bins, rows), BF16),
            pltpu.VMEM((bins, bins), BF16),
            pltpu.VMEM((bins, bins), BF16),
            pltpu.VMEM((groups, bins, chans), BF16),
            pltpu.VMEM((TABLE_ROWS, chans), F32),
            pltpu.SemaphoreType.DMA,
            pltpu.SemaphoreType.DMA((groups,)),
            pltpu.SemaphoreType.DMA((groups,)),
        ],
        compiler_params=pltpu.CompilerParams(
            collective_id=0, has_side_effects=True, vmem_limit_bytes=40 << 20
        ),
        name="chain",
    )(saved, top, weight, table, timesteps, dilations)


def reduce_kernel(
    scale, part_ref, out_ref,
    half_in, half, quarter_in, quarter, piece_in, piece, far_in,
    send_sem, recv_sem,
):
    dp = lax.axis_index("dp")
    core = dp % 2
    zpos = (dp // 2) % NZ
    ypos = (dp // (2 * NZ)) % NY
    xpos = dp // (2 * NZ * NY)
    side = NX
    half_rows, chans = half.shape
    quarter_rows = quarter.shape[0]
    width = piece.shape[1]

    def index_of(x, y, z, c):
        return ((x * NY + y) * NZ + z) * 2 + c

    first = xpos * (1 - core) + ypos * core
    second = ypos * (1 - core) + xpos * core

    def at(a, b):
        return index_of(a * (1 - core) + b * core, b * (1 - core) + a * core, zpos, core)

    mate = index_of(xpos, ypos, zpos, 1 - core)
    far = index_of(xpos, ypos, (zpos + 1) % NZ, core)
    peers_a = [(first + j) % side for j in range(1, side)]
    peers_b = [(second + j) % side for j in range(1, side)]
    everyone = [mate, far] + [at(a, second) for a in peers_a] + [at(first, b) for b in peers_b]

    barrier = pltpu.get_barrier_semaphore()
    for who in everyone:
        pl.semaphore_signal(barrier, inc=1, device_id={"dp": who}, device_id_type=MESH)
    pl.semaphore_wait(barrier, len(everyone))

    def send(src, dst, slot, who):
        copy = pltpu.make_async_remote_copy(
            src_ref=src, dst_ref=dst, send_sem=send_sem.at[slot], recv_sem=recv_sem.at[slot],
            device_id={"dp": who}, device_id_type=MESH,
        )
        copy.start()
        return copy

    def rows_at(start, size):
        return pl.ds(pl.multiple_of(start, 16), size)

    def cols_at(start, size):
        return pl.ds(pl.multiple_of(start, 128), size)

    def by_rows(count, step, body):
        def run(i, carry):
            body(pl.multiple_of(i * step, step))
            return carry
        lax.fori_loop(0, count // step, run, 0)

    pending = []
    copy = send(part_ref.at[rows_at((1 - core) * half_rows, half_rows), :], half_in, 0, mate)
    copy.wait_recv()
    pending.append(copy)

    def add_half(r):
        own = part_ref[pl.ds(pl.multiple_of(core * half_rows + r, 16), 16), :].astype(F32)
        half[pl.ds(r, 16), :] = (own + half_in[pl.ds(r, 16), :].astype(F32)).astype(BF16)
    by_rows(half_rows, 16, add_half)

    copies = [
        send(half.at[rows_at(a * quarter_rows, quarter_rows), :], quarter_in.at[j], 1 + j, at(a, second))
        for j, a in enumerate(peers_a)
    ]
    for copy in copies:
        copy.wait_recv()
    pending += copies

    def add_quarter(r):
        total = half[pl.ds(pl.multiple_of(first * quarter_rows + r, 16), 16), :].astype(F32)
        for j in range(side - 1):
            total += quarter_in[j, pl.ds(r, 16), :].astype(F32)
        quarter[pl.ds(r, 16), :] = total.astype(BF16)
    by_rows(quarter_rows, 16, add_quarter)

    copies = [
        send(quarter.at[:, cols_at(b * width, width)], piece_in.at[j], 4 + j, at(first, b))
        for j, b in enumerate(peers_b)
    ]
    for copy in copies:
        copy.wait_recv()
    pending += copies

    total = quarter[:, cols_at(second * width, width)].astype(F32)
    for j in range(side - 1):
        total += piece_in[j].astype(F32)
    piece[...] = total.astype(BF16)

    copy = send(piece, far_in, 7, far)
    copy.wait_recv()
    pending.append(copy)
    row_base = core * half_rows + first * quarter_rows
    mine = (rows_at(row_base, quarter_rows), cols_at(second * width, width))
    out_ref[mine] = ((piece[...].astype(F32) + far_in[...].astype(F32)) * scale).astype(BF16)

    copies = [
        send(out_ref.at[mine], out_ref.at[mine], 8 + j, at(first, b)) for j, b in enumerate(peers_b)
    ]
    for copy in copies:
        copy.wait_recv()
    pending += copies

    band = (rows_at(row_base, quarter_rows), slice(None))
    copies = [
        send(out_ref.at[band], out_ref.at[band], 11 + j, at(a, second)) for j, a in enumerate(peers_a)
    ]
    for copy in copies:
        copy.wait_recv()
    pending += copies

    block = (rows_at(core * half_rows, half_rows), slice(None))
    copy = send(out_ref.at[block], out_ref.at[block], 14, mate)
    copy.wait_recv()
    pending.append(copy)
    for copy in pending:
        copy.wait_send()


def reduce_all(part, scale):
    rows, chans = part.shape
    half, quarter, width = rows // 2, rows // 2 // NX, chans // NY
    vmem = pl.BlockSpec(memory_space=pltpu.VMEM)
    return pl.pallas_call(
        functools.partial(reduce_kernel, scale),
        out_shape=jax.ShapeDtypeStruct((rows, chans), BF16),
        in_specs=[vmem],
        out_specs=vmem,
        scratch_shapes=[
            pltpu.VMEM((half, chans), BF16),
            pltpu.VMEM((half, chans), BF16),
            pltpu.VMEM((NX - 1, quarter, chans), BF16),
            pltpu.VMEM((quarter, chans), BF16),
            pltpu.VMEM((NX - 1, quarter, width), BF16),
            pltpu.VMEM((quarter, width), BF16),
            pltpu.VMEM((quarter, width), BF16),
            pltpu.SemaphoreType.DMA((15,)),
            pltpu.SemaphoreType.DMA((15,)),
        ],
        compiler_params=pltpu.CompilerParams(
            collective_id=1, has_side_effects=True, vmem_limit_bytes=32 << 20
        ),
        name="reduce_all",
    )(part)


def body(section_input, top_grad, conv_weight, step_table, timesteps, dilations):
    taps, chans = conv_weight.shape[1], conv_weight.shape[2]
    groups, bins = top_grad.shape[0], top_grad.shape[1]
    weight = conv_weight.reshape(taps * chans, chans)
    grads, part = chain(section_input[0], top_grad, weight, step_table[0], timesteps, dilations)
    scale = 1.0 / math.sqrt(groups * lax.axis_size("dp") * bins)
    total = reduce_all(part, scale)
    weight_out = total[: taps * chans].reshape(1, taps, chans, chans)
    table_out = total[taps * chans : taps * chans + step_table.shape[1]][None]
    return grads[None], weight_out, table_out


def solution(mesh):
    placed = (
        P("section", "dp", None, None),
        P("dp", None, None),
        P("section", None, None, None),
        P("section", None, None),
        P("dp"),
        P("section"),
    )
    return jax.shard_map(
        body,
        mesh=mesh,
        in_specs=placed,
        out_specs=(
            P("section", "dp", None, None),
            P("section", None, None, None),
            P("section", None, None),
        ),
        check_vma=False,
    )
```

```python
import functools
import math

import jax
import jax.numpy as jnp
from jax import lax
from jax.experimental import pallas as pl
from jax.experimental.pallas import tpu as pltpu
from jax.sharding import PartitionSpec as P

MESH = pl.DeviceIdType.MESH
NX, NY, NZ = 4, 4, 2
TABLE_ROWS = 64
PAD_ROWS = 128
CHUNKS = ((0, 64), (64, 112), (112, 160), (160, 208))
STAGES = 10
F32 = jnp.float32
BF16 = jnp.bfloat16


def chain_kernel(
    x_ref, top_ref, w_ref, tab_ref, ts_ref, dil_ref, gout_ref, part_ref,
    wt, ht, fw, sp, bt, ups, downs, recv, tacc, top_sem, send_sem, recv_sem,
):
    sec = lax.axis_index("section")
    last = lax.axis_size("section") - 1
    groups, bins, chans = x_ref.shape
    steps = tab_ref.shape[0]
    dil = dil_ref[0]

    barrier = pltpu.get_barrier_semaphore()

    @pl.when(sec > 0)
    def _():
        pl.semaphore_signal(barrier, inc=1, device_id={"section": sec - 1}, device_id_type=MESH)

    @pl.when(sec < last)
    def _():
        pl.semaphore_signal(barrier, inc=1, device_id={"section": sec + 1}, device_id_type=MESH)

    top_copy = pltpu.make_async_copy(top_ref, recv, top_sem)

    @pl.when(sec == last)
    def _():
        top_copy.start()

    to_bin = lax.broadcasted_iota(jnp.int32, (bins, bins), 0)
    from_bin = lax.broadcasted_iota(jnp.int32, (bins, bins), 1)
    downs[...] = jnp.where(from_bin == to_bin - dil, 1.0, 0.0).astype(BF16)
    ups[...] = jnp.where(from_bin == to_bin + dil, 1.0, 0.0).astype(BF16)
    step_rows = lax.broadcasted_iota(jnp.int32, (steps, chans), 0)

    def mix(b, carry):
        row = pl.multiple_of(b * bins, bins)
        table = tab_ref[...].astype(F32)
        embed = jnp.sum(jnp.where(step_rows == ts_ref[b], table, 0.0), axis=0, keepdims=True)
        mixed = (x_ref[b].astype(F32) + embed).astype(BF16)
        fw[pl.ds(row, bins), chans : 2 * chans] = mixed
        fw[pl.ds(row, bins), 0:chans] = jnp.dot(
            downs[...], mixed, preferred_element_type=F32
        ).astype(BF16)
        fw[pl.ds(row, bins), 2 * chans :] = jnp.dot(
            ups[...], mixed, preferred_element_type=F32
        ).astype(BF16)
        return carry

    lax.fori_loop(0, groups, mix, 0)
    for c in range(0, chans, 256):
        preact = jnp.dot(fw[...], w_ref[:, c : c + 256], preferred_element_type=F32)
        gate = jax.nn.sigmoid(preact)
        sp[:, c : c + 256] = gate * (1.0 + preact * (1.0 - gate))
    for tap in range(3):
        wt[tap * chans : (tap + 1) * chans, :] = w_ref[tap * chans : (tap + 1) * chans, :].T
    tacc[...] = jnp.zeros_like(tacc)

    @pl.when(sec < last)
    def _():
        ht[...] = fw[:, chans : 2 * chans].T

    @pl.when(jnp.logical_and(sec > 0, sec < last))
    def _():
        pl.semaphore_wait(barrier, 2)

    @pl.when(jnp.logical_or(sec == 0, sec == last))
    def _():
        pl.semaphore_wait(barrier, 1)

    @pl.when(sec == last)
    def _():
        top_copy.wait()

    table_rows = lax.broadcasted_iota(jnp.int32, (TABLE_ROWS, chans), 0)

    def hop(b):
        return pltpu.make_async_remote_copy(
            src_ref=gout_ref.at[b],
            dst_ref=recv.at[b],
            send_sem=send_sem.at[b],
            recv_sem=recv_sem.at[b],
            device_id={"section": sec - 1},
            device_id_type=MESH,
        )

    def layer(b, carry):
        row = pl.multiple_of(b * bins, bins)

        @pl.when(sec < last)
        def _():
            hop(b).wait_recv()

        delta = (recv[b].astype(F32) * sp[pl.ds(row, bins), :]).astype(BF16)
        bt[pl.ds(row, bins), chans : 2 * chans] = delta
        bt[pl.ds(row, bins), 0:chans] = jnp.dot(
            ups[...], delta, preferred_element_type=F32
        ).astype(BF16)
        bt[pl.ds(row, bins), 2 * chans :] = jnp.dot(
            downs[...], delta, preferred_element_type=F32
        ).astype(BF16)
        grad = jnp.dot(bt[pl.ds(row, bins), :], wt[...], preferred_element_type=F32)
        gout_ref[b] = (recv[b].astype(F32) + grad).astype(BF16)

        @pl.when(sec > 0)
        def _():
            hop(b).start()

        total = jnp.sum(grad, axis=0, keepdims=True)
        tacc[...] += jnp.where(table_rows == ts_ref[b], total, 0.0)
        return carry

    lax.fori_loop(0, groups, layer, 0)

    @pl.when(sec == last)
    def _():
        ht[...] = fw[:, chans : 2 * chans].T

    rows = 3 * chans
    for tap in range(3):
        span = slice(tap * chans, (tap + 1) * chans)
        part_ref[span, :] = jnp.dot(ht[...], bt[:, span], preferred_element_type=F32).astype(BF16)
    part_ref[rows : rows + TABLE_ROWS, :] = tacc[...].astype(BF16)
    part_ref[rows + TABLE_ROWS :, :] = jnp.zeros((PAD_ROWS - TABLE_ROWS, chans), BF16)

    @pl.when(sec > 0)
    def _():
        for b in range(groups):
            hop(b).wait_send()


def chain(saved, top, weight, table, timesteps, dilations):
    groups, bins, chans = saved.shape
    vmem = pl.BlockSpec(memory_space=pltpu.VMEM)
    smem = pl.BlockSpec(memory_space=pltpu.SMEM)
    rows = 3 * chans
    return pl.pallas_call(
        chain_kernel,
        out_shape=(
            jax.ShapeDtypeStruct((groups, bins, chans), BF16),
            jax.ShapeDtypeStruct((rows + PAD_ROWS, chans), BF16),
        ),
        in_specs=[vmem, pl.BlockSpec(memory_space=pl.ANY), vmem, vmem, smem, smem],
        out_specs=(vmem, vmem),
        scratch_shapes=[
            pltpu.VMEM((rows, chans), BF16),
            pltpu.VMEM((chans, groups * bins), BF16),
            pltpu.VMEM((groups * bins, rows), BF16),
            pltpu.VMEM((groups * bins, chans), F32),
            pltpu.VMEM((groups * bins, rows), BF16),
            pltpu.VMEM((bins, bins), BF16),
            pltpu.VMEM((bins, bins), BF16),
            pltpu.VMEM((groups, bins, chans), BF16),
            pltpu.VMEM((TABLE_ROWS, chans), F32),
            pltpu.SemaphoreType.DMA,
            pltpu.SemaphoreType.DMA((groups,)),
            pltpu.SemaphoreType.DMA((groups,)),
        ],
        compiler_params=pltpu.CompilerParams(
            collective_id=0, has_side_effects=True, vmem_limit_bytes=40 << 20
        ),
        name="chain",
    )(saved, top, weight, table, timesteps, dilations)


def reduce_kernel(
    scale, part_ref, out_ref,
    half_in, half, relay_in, relay, near_in, next_in, quarter, piece_in, piece, far_in,
    send_sem, recv_sem,
):
    dp = lax.axis_index("dp")
    core = dp % 2
    zpos = (dp // 2) % NZ
    ypos = (dp // (2 * NZ)) % NY
    xpos = dp // (2 * NZ * NY)
    side = NX
    width = piece.shape[1]

    def index_of(x, y, z, c):
        return ((x * NY + y) * NZ + z) * 2 + c

    first = xpos * (1 - core) + ypos * core
    second = ypos * (1 - core) + xpos * core

    def at(a, b):
        return index_of(a * (1 - core) + b * core, b * (1 - core) + a * core, zpos, core)

    mate = index_of(xpos, ypos, zpos, 1 - core)
    far = index_of(xpos, ypos, (zpos + 1) % NZ, core)
    ahead, behind = (first + 1) % side, (first + side - 1) % side
    opposite = (first + 2) % side
    peers = [(second + j) % side for j in range(1, side)]
    everyone = [mate, far, at(ahead, second), at(behind, second)] + [at(first, b) for b in peers]

    barrier = pltpu.get_barrier_semaphore()
    for who in everyone:
        pl.semaphore_signal(barrier, inc=1, device_id={"dp": who}, device_id_type=MESH)
    pl.semaphore_wait(barrier, len(everyone))

    pending = []

    def send(src, dst, chunk, slot, who):
        copy = pltpu.make_async_remote_copy(
            src_ref=src, dst_ref=dst,
            send_sem=send_sem.at[chunk, slot], recv_sem=recv_sem.at[chunk, slot],
            device_id={"dp": who}, device_id_type=MESH,
        )
        copy.start()
        pending.append(copy)
        return copy

    def cols_at(start, size):
        return pl.ds(pl.multiple_of(start, 128), size)

    mine, theirs = core * side, (1 - core) * side
    own_cols = cols_at(second * width, width)

    def steps(chunk):
        start, stop = CHUNKS[chunk]
        rows = pl.ds(start, stop - start)
        onward, backward = (ahead, behind) if chunk % 2 == 0 else (behind, ahead)

        def forward_to_mate(slot, quarter_id):
            ref = out_ref.at[mine + quarter_id, rows, :]
            return send(ref, ref, chunk, slot, mate)

        copy = send(
            part_ref.at[pl.ds(theirs, side), rows, :], half_in.at[:, rows, :], chunk, 0, mate
        )
        yield
        copy.wait_recv()
        for q in range(side):
            own = part_ref[mine + q, rows, :].astype(F32)
            half[q, rows, :] = (own + half_in[q, rows, :].astype(F32)).astype(BF16)
        passed = send(
            half.at[opposite, rows, :], relay_in.at[rows, :], chunk, 1, at(onward, second)
        )
        direct = send(
            half.at[backward, rows, :], near_in.at[rows, :], chunk, 2, at(backward, second)
        )
        yield
        passed.wait_recv()
        relay[rows, :] = (
            half[onward, rows, :].astype(F32) + relay_in[rows, :].astype(F32)
        ).astype(BF16)
        joined = send(relay.at[rows, :], next_in.at[rows, :], chunk, 3, at(onward, second))
        yield
        direct.wait_recv()
        joined.wait_recv()
        quarter[rows, :] = (
            half[first, rows, :].astype(F32)
            + near_in[rows, :].astype(F32)
            + next_in[rows, :].astype(F32)
        ).astype(BF16)
        copies = [
            send(
                quarter.at[rows, cols_at(b * width, width)], piece_in.at[j, rows, :],
                chunk, 4 + j, at(first, b),
            )
            for j, b in enumerate(peers)
        ]
        yield
        for copy in copies:
            copy.wait_recv()
        total = quarter[rows, own_cols].astype(F32)
        for j in range(side - 1):
            total += piece_in[j, rows, :].astype(F32)
        piece[rows, :] = total.astype(BF16)
        copy = send(piece.at[rows, :], far_in.at[rows, :], chunk, 7, far)
        yield
        copy.wait_recv()
        out_ref[mine + first, rows, own_cols] = (
            (piece[rows, :].astype(F32) + far_in[rows, :].astype(F32)) * scale
        ).astype(BF16)
        block = out_ref.at[mine + first, rows, own_cols]
        copies = [send(block, block, chunk, 8 + j, at(first, b)) for j, b in enumerate(peers)]
        yield
        for copy in copies:
            copy.wait_recv()
        band = out_ref.at[mine + first, rows, :]
        one = send(band, band, chunk, 11, at(onward, second))
        two = send(band, band, chunk, 12, at(backward, second))
        final = [forward_to_mate(14, first)]
        yield
        one.wait_recv()
        band = out_ref.at[mine + backward, rows, :]
        three = send(band, band, chunk, 13, at(onward, second))
        final.append(forward_to_mate(15, backward))
        two.wait_recv()
        final.append(forward_to_mate(16, onward))
        yield
        three.wait_recv()
        final.append(forward_to_mate(17, opposite))
        yield
        for copy in final:
            copy.wait_recv()

    running = [steps(chunk) for chunk in range(len(CHUNKS))]
    for tick in range(STAGES + len(CHUNKS) - 1):
        for chunk, run in enumerate(running):
            if 0 <= tick - chunk < STAGES:
                next(run, None)
    for copy in pending:
        copy.wait_send()


def reduce_all(part, scale):
    quarters, rows, chans = part.shape
    width = chans // NY
    vmem = pl.BlockSpec(memory_space=pltpu.VMEM)
    return pl.pallas_call(
        functools.partial(reduce_kernel, scale),
        out_shape=jax.ShapeDtypeStruct(part.shape, BF16),
        in_specs=[vmem],
        out_specs=vmem,
        scratch_shapes=[
            pltpu.VMEM((NX, rows, chans), BF16),
            pltpu.VMEM((NX, rows, chans), BF16),
            pltpu.VMEM((rows, chans), BF16),
            pltpu.VMEM((rows, chans), BF16),
            pltpu.VMEM((rows, chans), BF16),
            pltpu.VMEM((rows, chans), BF16),
            pltpu.VMEM((rows, chans), BF16),
            pltpu.VMEM((NY - 1, rows, width), BF16),
            pltpu.VMEM((rows, width), BF16),
            pltpu.VMEM((rows, width), BF16),
            pltpu.SemaphoreType.DMA((len(CHUNKS), 18)),
            pltpu.SemaphoreType.DMA((len(CHUNKS), 18)),
        ],
        compiler_params=pltpu.CompilerParams(
            collective_id=1, has_side_effects=True, vmem_limit_bytes=32 << 20
        ),
        name="reduce_all",
    )(part)


def body(section_input, top_grad, conv_weight, step_table, timesteps, dilations):
    taps, chans = conv_weight.shape[1], conv_weight.shape[2]
    groups, bins = top_grad.shape[0], top_grad.shape[1]
    weight = conv_weight.reshape(taps * chans, chans)
    grads, part = chain(section_input[0], top_grad, weight, step_table[0], timesteps, dilations)
    scale = 1.0 / math.sqrt(groups * lax.axis_size("dp") * bins)
    total = reduce_all(part.reshape(2 * NX, -1, chans), scale).reshape(-1, chans)
    weight_out = total[: taps * chans].reshape(1, taps, chans, chans)
    table_out = total[taps * chans : taps * chans + step_table.shape[1]][None]
    return grads[None], weight_out, table_out


def solution(mesh):
    placed = (
        P("section", "dp", None, None),
        P("dp", None, None),
        P("section", None, None, None),
        P("section", None, None),
        P("dp"),
        P("section"),
    )
    return jax.shard_map(
        body,
        mesh=mesh,
        in_specs=placed,
        out_specs=(
            P("section", "dp", None, None),
            P("section", None, None, None),
            P("section", None, None),
        ),
        check_vma=False,
    )
```

```python
import functools
import math

import jax
import jax.numpy as jnp
from jax import lax
from jax.experimental import pallas as pl
from jax.experimental.pallas import tpu as pltpu
from jax.sharding import PartitionSpec as P

MESH = pl.DeviceIdType.MESH
NX, NY, NZ = 4, 4, 2
TABLE_ROWS = 64
PAD_ROWS = 128
CHUNKS = ((0, 64), (64, 112), (112, 160), (160, 208))
STAGES = 10
F32 = jnp.float32
BF16 = jnp.bfloat16


def chain_kernel(
    x_hbm, top_hbm, w_hbm, tab_hbm, ts_ref, dil_ref, gout_ref, part_ref,
    x_ref, w_ref, tab_ref, wt, ht, fw, sp, bt, ups, downs, recv, tacc,
    load_sem, send_sem, recv_sem,
):
    sec = lax.axis_index("section")
    last = lax.axis_size("section") - 1
    groups, bins, chans = x_ref.shape
    steps = tab_ref.shape[0]
    dil = dil_ref[0]

    barrier = pltpu.get_barrier_semaphore()

    @pl.when(sec > 0)
    def _():
        pl.semaphore_signal(barrier, inc=1, device_id={"section": sec - 1}, device_id_type=MESH)

    @pl.when(sec < last)
    def _():
        pl.semaphore_signal(barrier, inc=1, device_id={"section": sec + 1}, device_id_type=MESH)

    table_copy = pltpu.make_async_copy(tab_hbm, tab_ref, load_sem.at[0])
    x_copy = pltpu.make_async_copy(x_hbm, x_ref, load_sem.at[1])
    weight_copy = pltpu.make_async_copy(w_hbm, w_ref, load_sem.at[2])
    top_copy = pltpu.make_async_copy(top_hbm, recv, load_sem.at[3])
    table_copy.start()
    x_copy.start()
    weight_copy.start()

    @pl.when(sec == last)
    def _():
        top_copy.start()

    to_bin = lax.broadcasted_iota(jnp.int32, (bins, bins), 0)
    from_bin = lax.broadcasted_iota(jnp.int32, (bins, bins), 1)
    downs[...] = jnp.where(from_bin == to_bin - dil, 1.0, 0.0).astype(BF16)
    ups[...] = jnp.where(from_bin == to_bin + dil, 1.0, 0.0).astype(BF16)
    step_rows = lax.broadcasted_iota(jnp.int32, (steps, chans), 0)

    def mix(b, carry):
        row = pl.multiple_of(b * bins, bins)
        table = tab_ref[...].astype(F32)
        embed = jnp.sum(jnp.where(step_rows == ts_ref[b], table, 0.0), axis=0, keepdims=True)
        mixed = (x_ref[b].astype(F32) + embed).astype(BF16)
        fw[pl.ds(row, bins), chans : 2 * chans] = mixed
        fw[pl.ds(row, bins), 0:chans] = jnp.dot(
            downs[...], mixed, preferred_element_type=F32
        ).astype(BF16)
        fw[pl.ds(row, bins), 2 * chans :] = jnp.dot(
            ups[...], mixed, preferred_element_type=F32
        ).astype(BF16)
        return carry

    table_copy.wait()
    x_copy.wait()
    lax.fori_loop(0, groups, mix, 0)
    weight_copy.wait()
    for c in range(0, chans, 256):
        preact = jnp.dot(fw[...], w_ref[:, c : c + 256], preferred_element_type=F32)
        gate = jax.nn.sigmoid(preact)
        sp[:, c : c + 256] = gate * (1.0 + preact * (1.0 - gate))
    for tap in range(3):
        wt[tap * chans : (tap + 1) * chans, :] = w_ref[tap * chans : (tap + 1) * chans, :].T
    tacc[...] = jnp.zeros_like(tacc)

    @pl.when(sec < last)
    def _():
        ht[...] = fw[:, chans : 2 * chans].T

    @pl.when(jnp.logical_and(sec > 0, sec < last))
    def _():
        pl.semaphore_wait(barrier, 2)

    @pl.when(jnp.logical_or(sec == 0, sec == last))
    def _():
        pl.semaphore_wait(barrier, 1)

    @pl.when(sec == last)
    def _():
        top_copy.wait()

    table_rows = lax.broadcasted_iota(jnp.int32, (TABLE_ROWS, chans // 2), 0)

    half = chans // 2

    def hop(b, h):
        span = pl.ds(h * half, half)
        return pltpu.make_async_remote_copy(
            src_ref=gout_ref.at[b, :, span],
            dst_ref=recv.at[b, :, span],
            send_sem=send_sem.at[b, h],
            recv_sem=recv_sem.at[b, h],
            device_id={"section": sec - 1},
            device_id_type=MESH,
        )

    def layer(b, carry):
        rows = pl.ds(pl.multiple_of(b * bins, bins), bins)
        for h in range(2):
            lo, hi = h * half, (h + 1) * half

            @pl.when(sec < last)
            def _():
                hop(b, h).wait_recv()

            delta = (recv[b, :, lo:hi].astype(F32) * sp[rows, lo:hi]).astype(BF16)
            bt[rows, chans + lo : chans + hi] = delta
            bt[rows, lo:hi] = jnp.dot(
                ups[...], delta, preferred_element_type=F32
            ).astype(BF16)
            bt[rows, 2 * chans + lo : 2 * chans + hi] = jnp.dot(
                downs[...], delta, preferred_element_type=F32
            ).astype(BF16)
        for h in range(2):
            lo, hi = h * half, (h + 1) * half
            grad = jnp.dot(bt[rows, :], wt[:, lo:hi], preferred_element_type=F32)
            gout_ref[b, :, lo:hi] = (recv[b, :, lo:hi].astype(F32) + grad).astype(BF16)

            @pl.when(sec > 0)
            def _():
                hop(b, h).start()

            total = jnp.sum(grad, axis=0, keepdims=True)
            tacc[:, lo:hi] += jnp.where(table_rows == ts_ref[b], total, 0.0)
        return carry

    lax.fori_loop(0, groups, layer, 0)

    @pl.when(sec == last)
    def _():
        ht[...] = fw[:, chans : 2 * chans].T

    rows = 3 * chans
    for tap in range(3):
        span = slice(tap * chans, (tap + 1) * chans)
        part_ref[span, :] = jnp.dot(ht[...], bt[:, span], preferred_element_type=F32).astype(BF16)
    part_ref[rows : rows + TABLE_ROWS, :] = tacc[...].astype(BF16)
    part_ref[rows + TABLE_ROWS :, :] = jnp.zeros((PAD_ROWS - TABLE_ROWS, chans), BF16)

    @pl.when(sec > 0)
    def _():
        for b in range(groups):
            for h in range(2):
                hop(b, h).wait_send()


def chain(saved, top, weight, table, timesteps, dilations):
    groups, bins, chans = saved.shape
    vmem = pl.BlockSpec(memory_space=pltpu.VMEM)
    hbm = pl.BlockSpec(memory_space=pltpu.HBM)
    smem = pl.BlockSpec(memory_space=pltpu.SMEM)
    rows = 3 * chans
    return pl.pallas_call(
        chain_kernel,
        out_shape=(
            jax.ShapeDtypeStruct((groups, bins, chans), BF16),
            jax.ShapeDtypeStruct((rows + PAD_ROWS, chans), BF16),
        ),
        in_specs=[hbm, hbm, hbm, hbm, smem, smem],
        out_specs=(vmem, vmem),
        scratch_shapes=[
            pltpu.VMEM(saved.shape, BF16),
            pltpu.VMEM(weight.shape, BF16),
            pltpu.VMEM(table.shape, BF16),
            pltpu.VMEM((rows, chans), BF16),
            pltpu.VMEM((chans, groups * bins), BF16),
            pltpu.VMEM((groups * bins, rows), BF16),
            pltpu.VMEM((groups * bins, chans), F32),
            pltpu.VMEM((groups * bins, rows), BF16),
            pltpu.VMEM((bins, bins), BF16),
            pltpu.VMEM((bins, bins), BF16),
            pltpu.VMEM((groups, bins, chans), BF16),
            pltpu.VMEM((TABLE_ROWS, chans), F32),
            pltpu.SemaphoreType.DMA((4,)),
            pltpu.SemaphoreType.DMA((groups, 2)),
            pltpu.SemaphoreType.DMA((groups, 2)),
        ],
        compiler_params=pltpu.CompilerParams(
            collective_id=0, has_side_effects=True, vmem_limit_bytes=67043328
        ),
        name="chain",
    )(saved, top, weight, table, timesteps, dilations)


def reduce_kernel(
    scale, part_ref, out_ref,
    half_in, half, relay_in, relay, near_in, next_in, quarter, piece_in, piece, far_in,
    send_sem, recv_sem,
):
    dp = lax.axis_index("dp")
    core = dp % 2
    zpos = (dp // 2) % NZ
    ypos = (dp // (2 * NZ)) % NY
    xpos = dp // (2 * NZ * NY)
    side = NX
    width = piece.shape[1]

    def index_of(x, y, z, c):
        return ((x * NY + y) * NZ + z) * 2 + c

    first = xpos * (1 - core) + ypos * core
    second = ypos * (1 - core) + xpos * core

    def at(a, b):
        return index_of(a * (1 - core) + b * core, b * (1 - core) + a * core, zpos, core)

    mate = index_of(xpos, ypos, zpos, 1 - core)
    far = index_of(xpos, ypos, (zpos + 1) % NZ, core)
    ahead, behind = (first + 1) % side, (first + side - 1) % side
    opposite = (first + 2) % side
    peers = [(second + j) % side for j in range(1, side)]
    everyone = [mate, far, at(ahead, second), at(behind, second)] + [at(first, b) for b in peers]

    barrier = pltpu.get_barrier_semaphore()
    for who in everyone:
        pl.semaphore_signal(barrier, inc=1, device_id={"dp": who}, device_id_type=MESH)
    pl.semaphore_wait(barrier, len(everyone))

    pending = []

    def send(src, dst, chunk, slot, who):
        copy = pltpu.make_async_remote_copy(
            src_ref=src, dst_ref=dst,
            send_sem=send_sem.at[chunk, slot], recv_sem=recv_sem.at[chunk, slot],
            device_id={"dp": who}, device_id_type=MESH,
        )
        copy.start()
        pending.append(copy)
        return copy

    def cols_at(start, size):
        return pl.ds(pl.multiple_of(start, 128), size)

    mine, theirs = core * side, (1 - core) * side
    own_cols = cols_at(second * width, width)

    def steps(chunk):
        start, stop = CHUNKS[chunk]
        rows = pl.ds(start, stop - start)
        onward, backward = (ahead, behind) if chunk % 2 == 0 else (behind, ahead)

        def forward_to_mate(slot, quarter_id):
            ref = out_ref.at[mine + quarter_id, rows, :]
            return send(ref, ref, chunk, slot, mate)

        copy = send(
            part_ref.at[pl.ds(theirs, side), rows, :], half_in.at[:, rows, :], chunk, 0, mate
        )
        yield
        copy.wait_recv()
        for q in range(side):
            own = part_ref[mine + q, rows, :].astype(F32)
            half[q, rows, :] = (own + half_in[q, rows, :].astype(F32)).astype(BF16)
        passed = send(
            half.at[opposite, rows, :], relay_in.at[rows, :], chunk, 1, at(onward, second)
        )
        direct = send(
            half.at[backward, rows, :], near_in.at[rows, :], chunk, 2, at(backward, second)
        )
        yield
        passed.wait_recv()
        relay[rows, :] = (
            half[onward, rows, :].astype(F32) + relay_in[rows, :].astype(F32)
        ).astype(BF16)
        joined = send(relay.at[rows, :], next_in.at[rows, :], chunk, 3, at(onward, second))
        yield
        direct.wait_recv()
        joined.wait_recv()
        quarter[rows, :] = (
            half[first, rows, :].astype(F32)
            + near_in[rows, :].astype(F32)
            + next_in[rows, :].astype(F32)
        ).astype(BF16)
        copies = [
            send(
                quarter.at[rows, cols_at(b * width, width)], piece_in.at[j, rows, :],
                chunk, 4 + j, at(first, b),
            )
            for j, b in enumerate(peers)
        ]
        yield
        for copy in copies:
            copy.wait_recv()
        total = quarter[rows, own_cols].astype(F32)
        for j in range(side - 1):
            total += piece_in[j, rows, :].astype(F32)
        piece[rows, :] = total.astype(BF16)
        copy = send(piece.at[rows, :], far_in.at[rows, :], chunk, 7, far)
        yield
        copy.wait_recv()
        out_ref[mine + first, rows, own_cols] = (
            (piece[rows, :].astype(F32) + far_in[rows, :].astype(F32)) * scale
        ).astype(BF16)
        block = out_ref.at[mine + first, rows, own_cols]
        copies = [send(block, block, chunk, 8 + j, at(first, b)) for j, b in enumerate(peers)]
        yield
        for copy in copies:
            copy.wait_recv()
        band = out_ref.at[mine + first, rows, :]
        one = send(band, band, chunk, 11, at(onward, second))
        two = send(band, band, chunk, 12, at(backward, second))
        final = [forward_to_mate(14, first)]
        yield
        one.wait_recv()
        band = out_ref.at[mine + backward, rows, :]
        three = send(band, band, chunk, 13, at(onward, second))
        final.append(forward_to_mate(15, backward))
        two.wait_recv()
        final.append(forward_to_mate(16, onward))
        yield
        three.wait_recv()
        final.append(forward_to_mate(17, opposite))
        yield
        for copy in final:
            copy.wait_recv()

    running = [steps(chunk) for chunk in range(len(CHUNKS))]
    for stage in range(STAGES):
        for run in running:
            next(run, None)
    for copy in pending:
        copy.wait_send()


def reduce_all(part, scale):
    quarters, rows, chans = part.shape
    width = chans // NY
    vmem = pl.BlockSpec(memory_space=pltpu.VMEM)
    return pl.pallas_call(
        functools.partial(reduce_kernel, scale),
        out_shape=jax.ShapeDtypeStruct(part.shape, BF16),
        in_specs=[vmem],
        out_specs=vmem,
        scratch_shapes=[
            pltpu.VMEM((NX, rows, chans), BF16),
            pltpu.VMEM((NX, rows, chans), BF16),
            pltpu.VMEM((rows, chans), BF16),
            pltpu.VMEM((rows, chans), BF16),
            pltpu.VMEM((rows, chans), BF16),
            pltpu.VMEM((rows, chans), BF16),
            pltpu.VMEM((rows, chans), BF16),
            pltpu.VMEM((NY - 1, rows, width), BF16),
            pltpu.VMEM((rows, width), BF16),
            pltpu.VMEM((rows, width), BF16),
            pltpu.SemaphoreType.DMA((len(CHUNKS), 18)),
            pltpu.SemaphoreType.DMA((len(CHUNKS), 18)),
        ],
        compiler_params=pltpu.CompilerParams(
            collective_id=1, has_side_effects=True, vmem_limit_bytes=32 << 20
        ),
        name="reduce_all",
    )(part)


def body(section_input, top_grad, conv_weight, step_table, timesteps, dilations):
    taps, chans = conv_weight.shape[1], conv_weight.shape[2]
    groups, bins = top_grad.shape[0], top_grad.shape[1]
    weight = conv_weight.reshape(taps * chans, chans)
    grads, part = chain(section_input[0], top_grad, weight, step_table[0], timesteps, dilations)
    scale = 1.0 / math.sqrt(groups * lax.axis_size("dp") * bins)
    total = reduce_all(part.reshape(2 * NX, -1, chans), scale).reshape(-1, chans)
    weight_out = total[: taps * chans].reshape(1, taps, chans, chans)
    table_out = total[taps * chans : taps * chans + step_table.shape[1]][None]
    return grads[None], weight_out, table_out


def solution(mesh):
    placed = (
        P("section", "dp", None, None),
        P("dp", None, None),
        P("section", None, None, None),
        P("section", None, None),
        P("dp"),
        P("section"),
    )
    return jax.shard_map(
        body,
        mesh=mesh,
        in_specs=placed,
        out_specs=(
            P("section", "dp", None, None),
            P("section", None, None, None),
            P("section", None, None),
        ),
        check_vma=False,
    )
```

```python
import functools
import math

import jax
import jax.numpy as jnp
from jax import lax
from jax.experimental import pallas as pl
from jax.experimental.pallas import tpu as pltpu
from jax.sharding import PartitionSpec as P

MESH = pl.DeviceIdType.MESH
NX, NY, NZ = 4, 4, 2
TABLE_ROWS = 64
PAD_ROWS = 128
CHUNKS = ((0, 64), (64, 112), (112, 160), (160, 208))
STAGES = 10
F32 = jnp.float32
BF16 = jnp.bfloat16


def chain_part(
    greeted, x_hbm, top_hbm, w_hbm, tab_hbm, ts_ref, dil_ref, gout_ref, part_ref,
    x_ref, w_ref, tab_ref, wt, ht, fw, sp, bt, ups, downs, recv, tacc,
    load_sem, send_sem, recv_sem,
):
    sec = lax.axis_index("section")
    last = lax.axis_size("section") - 1
    core = lax.axis_index("dp") % 2
    groups, bins, chans = x_ref.shape
    steps = tab_ref.shape[0]
    dil = dil_ref[0]

    barrier = pltpu.get_barrier_semaphore()

    @pl.when(sec > 0)
    def _():
        pl.semaphore_signal(barrier, inc=1, device_id={"section": sec - 1}, device_id_type=MESH)

    @pl.when(sec < last)
    def _():
        pl.semaphore_signal(barrier, inc=1, device_id={"section": sec + 1}, device_id_type=MESH)

    table_copy = pltpu.make_async_copy(tab_hbm, tab_ref, load_sem.at[0])
    x_copy = pltpu.make_async_copy(x_hbm, x_ref, load_sem.at[1])
    weight_copy = pltpu.make_async_copy(w_hbm, w_ref, load_sem.at[2])
    top_copy = pltpu.make_async_copy(top_hbm, recv, load_sem.at[3])
    table_copy.start()
    x_copy.start()
    weight_copy.start()

    @pl.when(sec == last)
    def _():
        top_copy.start()

    to_bin = lax.broadcasted_iota(jnp.int32, (bins, bins), 0)
    from_bin = lax.broadcasted_iota(jnp.int32, (bins, bins), 1)
    downs[...] = jnp.where(from_bin == to_bin - dil, 1.0, 0.0).astype(BF16)
    ups[...] = jnp.where(from_bin == to_bin + dil, 1.0, 0.0).astype(BF16)
    step_rows = lax.broadcasted_iota(jnp.int32, (steps, chans), 0)

    def mix(b, carry):
        row = pl.multiple_of(b * bins, bins)
        table = tab_ref[...].astype(F32)
        embed = jnp.sum(jnp.where(step_rows == ts_ref[b], table, 0.0), axis=0, keepdims=True)
        mixed = (x_ref[b].astype(F32) + embed).astype(BF16)
        fw[pl.ds(row, bins), chans : 2 * chans] = mixed
        fw[pl.ds(row, bins), 0:chans] = jnp.dot(
            downs[...], mixed, preferred_element_type=F32
        ).astype(BF16)
        fw[pl.ds(row, bins), 2 * chans :] = jnp.dot(
            ups[...], mixed, preferred_element_type=F32
        ).astype(BF16)
        return carry

    table_copy.wait()
    x_copy.wait()
    lax.fori_loop(0, groups, mix, 0)
    weight_copy.wait()
    for c in range(0, chans, 256):
        preact = jnp.dot(fw[...], w_ref[:, c : c + 256], preferred_element_type=F32)
        gate = jax.nn.sigmoid(preact)
        sp[:, c : c + 256] = gate * (1.0 + preact * (1.0 - gate))
    for tap in range(3):
        wt[tap * chans : (tap + 1) * chans, :] = w_ref[tap * chans : (tap + 1) * chans, :].T
    tacc[...] = jnp.zeros_like(tacc)

    @pl.when(jnp.logical_or(sec < last, core == 1))
    def _():
        ht[...] = fw[:, chans : 2 * chans].T

    @pl.when(jnp.logical_and(sec > 0, sec < last))
    def _():
        pl.semaphore_wait(barrier, greeted + 2)

    @pl.when(jnp.logical_or(sec == 0, sec == last))
    def _():
        pl.semaphore_wait(barrier, greeted + 1)

    @pl.when(sec == last)
    def _():
        top_copy.wait()

    table_rows = lax.broadcasted_iota(jnp.int32, (TABLE_ROWS, chans // 2), 0)

    half = chans // 2

    def hop(b, h):
        span = pl.ds(h * half, half)
        return pltpu.make_async_remote_copy(
            src_ref=gout_ref.at[b, :, span],
            dst_ref=recv.at[b, :, span],
            send_sem=send_sem.at[b, h],
            recv_sem=recv_sem.at[b, h],
            device_id={"section": sec - 1},
            device_id_type=MESH,
        )

    def layer(b, carry):
        rows = pl.ds(pl.multiple_of(b * bins, bins), bins)
        for h in range(2):
            lo, hi = h * half, (h + 1) * half

            @pl.when(sec < last)
            def _():
                hop(b, h).wait_recv()

            delta = (recv[b, :, lo:hi].astype(F32) * sp[rows, lo:hi]).astype(BF16)
            bt[rows, chans + lo : chans + hi] = delta
            bt[rows, lo:hi] = jnp.dot(
                ups[...], delta, preferred_element_type=F32
            ).astype(BF16)
            bt[rows, 2 * chans + lo : 2 * chans + hi] = jnp.dot(
                downs[...], delta, preferred_element_type=F32
            ).astype(BF16)
        for h in range(2):
            lo, hi = h * half, (h + 1) * half
            grad = jnp.dot(bt[rows, :], wt[:, lo:hi], preferred_element_type=F32)
            gout_ref[b, :, lo:hi] = (recv[b, :, lo:hi].astype(F32) + grad).astype(BF16)

            @pl.when(sec > 0)
            def _():
                hop(b, h).start()

            total = jnp.sum(grad, axis=0, keepdims=True)
            tacc[:, lo:hi] += jnp.where(table_rows == ts_ref[b], total, 0.0)
        return carry

    lax.fori_loop(0, groups, layer, 0)

    @pl.when(jnp.logical_and(sec == last, core == 0))
    def _():
        ht[...] = fw[:, chans : 2 * chans].T

    quarter_rows = part_ref.shape[1]

    def put(base, value):
        done = 0
        while done < value.shape[0]:
            q, r = divmod(base + done, quarter_rows)
            size = min(value.shape[0] - done, quarter_rows - r)
            part_ref[q, r : r + size, :] = value[done : done + size, :]
            done += size

    for tap in range(3):
        span = slice(tap * chans, (tap + 1) * chans)
        put(tap * chans, jnp.dot(ht[...], bt[:, span], preferred_element_type=F32).astype(BF16))
    put(3 * chans, tacc[...].astype(BF16))
    put(3 * chans + TABLE_ROWS, jnp.zeros((PAD_ROWS - TABLE_ROWS, chans), BF16))

    @pl.when(sec > 0)
    def _():
        for b in range(groups):
            for h in range(2):
                hop(b, h).wait_send()


def reduce_part(
    scale, run_chain, part_ref, out_ref,
    half_in, half, relay_in, relay, near_in, next_in, quarter, piece_in, piece, far_in,
    send_sem, recv_sem,
):
    dp = lax.axis_index("dp")
    core = dp % 2
    zpos = (dp // 2) % NZ
    ypos = (dp // (2 * NZ)) % NY
    xpos = dp // (2 * NZ * NY)
    side = NX
    width = piece.shape[1]

    def index_of(x, y, z, c):
        return ((x * NY + y) * NZ + z) * 2 + c

    first = xpos * (1 - core) + ypos * core
    second = ypos * (1 - core) + xpos * core

    def at(a, b):
        return index_of(a * (1 - core) + b * core, b * (1 - core) + a * core, zpos, core)

    mate = index_of(xpos, ypos, zpos, 1 - core)
    far = index_of(xpos, ypos, (zpos + 1) % NZ, core)
    ahead, behind = (first + 1) % side, (first + side - 1) % side
    opposite = (first + 2) % side
    peers = [(second + j) % side for j in range(1, side)]
    everyone = [mate, far, at(ahead, second), at(behind, second)] + [at(first, b) for b in peers]

    barrier = pltpu.get_barrier_semaphore()
    for who in everyone:
        pl.semaphore_signal(barrier, inc=1, device_id={"dp": who}, device_id_type=MESH)
    run_chain(len(everyone))

    pending = []

    def send(src, dst, chunk, slot, who):
        copy = pltpu.make_async_remote_copy(
            src_ref=src, dst_ref=dst,
            send_sem=send_sem.at[chunk, slot], recv_sem=recv_sem.at[chunk, slot],
            device_id={"dp": who}, device_id_type=MESH,
        )
        copy.start()
        pending.append(copy)
        return copy

    def cols_at(start, size):
        return pl.ds(pl.multiple_of(start, 128), size)

    mine, theirs = core * side, (1 - core) * side
    own_cols = cols_at(second * width, width)

    def steps(chunk):
        start, stop = CHUNKS[chunk]
        rows = pl.ds(start, stop - start)
        onward, backward = (ahead, behind) if chunk % 2 == 0 else (behind, ahead)

        def forward_to_mate(slot, quarter_id):
            ref = out_ref.at[mine + quarter_id, rows, :]
            return send(ref, ref, chunk, slot, mate)

        copy = send(
            part_ref.at[pl.ds(theirs, side), rows, :], half_in.at[:, rows, :], chunk, 0, mate
        )
        yield
        copy.wait_recv()
        for q in range(side):
            own = part_ref[mine + q, rows, :].astype(F32)
            half[q, rows, :] = (own + half_in[q, rows, :].astype(F32)).astype(BF16)
        passed = send(
            half.at[opposite, rows, :], relay_in.at[rows, :], chunk, 1, at(onward, second)
        )
        direct = send(
            half.at[backward, rows, :], near_in.at[rows, :], chunk, 2, at(backward, second)
        )
        yield
        passed.wait_recv()
        relay[rows, :] = (
            half[onward, rows, :].astype(F32) + relay_in[rows, :].astype(F32)
        ).astype(BF16)
        joined = send(relay.at[rows, :], next_in.at[rows, :], chunk, 3, at(onward, second))
        yield
        direct.wait_recv()
        joined.wait_recv()
        quarter[rows, :] = (
            half[first, rows, :].astype(F32)
            + near_in[rows, :].astype(F32)
            + next_in[rows, :].astype(F32)
        ).astype(BF16)
        copies = [
            send(
                quarter.at[rows, cols_at(b * width, width)], piece_in.at[j, rows, :],
                chunk, 4 + j, at(first, b),
            )
            for j, b in enumerate(peers)
        ]
        yield
        for copy in copies:
            copy.wait_recv()
        total = quarter[rows, own_cols].astype(F32)
        for j in range(side - 1):
            total += piece_in[j, rows, :].astype(F32)
        piece[rows, :] = total.astype(BF16)
        copy = send(piece.at[rows, :], far_in.at[rows, :], chunk, 7, far)
        yield
        copy.wait_recv()
        out_ref[mine + first, rows, own_cols] = (
            (piece[rows, :].astype(F32) + far_in[rows, :].astype(F32)) * scale
        ).astype(BF16)
        block = out_ref.at[mine + first, rows, own_cols]
        copies = [send(block, block, chunk, 8 + j, at(first, b)) for j, b in enumerate(peers)]
        yield
        for copy in copies:
            copy.wait_recv()
        band = out_ref.at[mine + first, rows, :]
        one = send(band, band, chunk, 11, at(onward, second))
        two = send(band, band, chunk, 12, at(backward, second))
        final = [forward_to_mate(14, first)]
        yield
        one.wait_recv()
        band = out_ref.at[mine + backward, rows, :]
        three = send(band, band, chunk, 13, at(onward, second))
        final.append(forward_to_mate(15, backward))
        two.wait_recv()
        final.append(forward_to_mate(16, onward))
        yield
        three.wait_recv()
        final.append(forward_to_mate(17, opposite))
        yield
        for copy in final:
            copy.wait_recv()

    running = [steps(chunk) for chunk in range(len(CHUNKS))]
    for stage in range(STAGES):
        for run in running:
            next(run, None)
    for copy in pending:
        copy.wait_send()


def kernel(scale, *refs):
    operands, (gout_hbm, out_ref), scratch = refs[:6], refs[6:8], refs[8:]
    gout_ref, part_ref, out_sem = scratch[:3]
    chain_scratch, reduce_scratch = scratch[3:18], scratch[18:]
    gout_copy = pltpu.make_async_copy(gout_ref, gout_hbm, out_sem)

    def run_chain(greeted):
        chain_part(greeted, *operands, gout_ref, part_ref, *chain_scratch)
        gout_copy.start()

    reduce_part(scale, run_chain, part_ref, out_ref, *reduce_scratch)
    gout_copy.wait()


def backward(saved, top, weight, table, timesteps, dilations, scale):
    groups, bins, chans = saved.shape
    vmem = pl.BlockSpec(memory_space=pltpu.VMEM)
    hbm = pl.BlockSpec(memory_space=pltpu.HBM)
    smem = pl.BlockSpec(memory_space=pltpu.SMEM)
    taps = 3 * chans
    rows = (taps + PAD_ROWS) // (2 * NX)
    width = chans // NY
    return pl.pallas_call(
        functools.partial(kernel, scale),
        out_shape=(
            jax.ShapeDtypeStruct((groups, bins, chans), BF16),
            jax.ShapeDtypeStruct((2 * NX, rows, chans), BF16),
        ),
        in_specs=[hbm, hbm, hbm, hbm, smem, smem],
        out_specs=(hbm, vmem),
        scratch_shapes=[
            pltpu.VMEM((groups, bins, chans), BF16),
            pltpu.VMEM((2 * NX, rows, chans), BF16),
            pltpu.SemaphoreType.DMA,
            pltpu.VMEM(saved.shape, BF16),
            pltpu.VMEM(weight.shape, BF16),
            pltpu.VMEM(table.shape, BF16),
            pltpu.VMEM((taps, chans), BF16),
            pltpu.VMEM((chans, groups * bins), BF16),
            pltpu.VMEM((groups * bins, taps), BF16),
            pltpu.VMEM((groups * bins, chans), F32),
            pltpu.VMEM((groups * bins, taps), BF16),
            pltpu.VMEM((bins, bins), BF16),
            pltpu.VMEM((bins, bins), BF16),
            pltpu.VMEM((groups, bins, chans), BF16),
            pltpu.VMEM((TABLE_ROWS, chans), F32),
            pltpu.SemaphoreType.DMA((4,)),
            pltpu.SemaphoreType.DMA((groups, 2)),
            pltpu.SemaphoreType.DMA((groups, 2)),
            pltpu.VMEM((NX, rows, chans), BF16),
            pltpu.VMEM((NX, rows, chans), BF16),
            pltpu.VMEM((rows, chans), BF16),
            pltpu.VMEM((rows, chans), BF16),
            pltpu.VMEM((rows, chans), BF16),
            pltpu.VMEM((rows, chans), BF16),
            pltpu.VMEM((rows, chans), BF16),
            pltpu.VMEM((NY - 1, rows, width), BF16),
            pltpu.VMEM((rows, width), BF16),
            pltpu.VMEM((rows, width), BF16),
            pltpu.SemaphoreType.DMA((len(CHUNKS), 18)),
            pltpu.SemaphoreType.DMA((len(CHUNKS), 18)),
        ],
        compiler_params=pltpu.CompilerParams(
            collective_id=0, has_side_effects=True, vmem_limit_bytes=67043328
        ),
        name="backward",
    )(saved, top, weight, table, timesteps, dilations)


def body(section_input, top_grad, conv_weight, step_table, timesteps, dilations):
    taps, chans = conv_weight.shape[1], conv_weight.shape[2]
    groups, bins = top_grad.shape[0], top_grad.shape[1]
    weight = conv_weight.reshape(taps * chans, chans)
    scale = 1.0 / math.sqrt(groups * lax.axis_size("dp") * bins)
    grads, total = backward(
        section_input[0], top_grad, weight, step_table[0], timesteps, dilations, scale
    )
    total = total.reshape(-1, chans)
    weight_out = total[: taps * chans].reshape(1, taps, chans, chans)
    table_out = total[taps * chans : taps * chans + step_table.shape[1]][None]
    return grads[None], weight_out, table_out


def solution(mesh):
    placed = (
        P("section", "dp", None, None),
        P("dp", None, None),
        P("section", None, None, None),
        P("section", None, None),
        P("dp"),
        P("section"),
    )
    return jax.shard_map(
        body,
        mesh=mesh,
        in_specs=placed,
        out_specs=(
            P("section", "dp", None, None),
            P("section", None, None, None),
            P("section", None, None),
        ),
        check_vma=False,
    )
```

```python
import functools
import math

import jax
import jax.numpy as jnp
from jax import lax
from jax.experimental import pallas as pl
from jax.experimental.pallas import tpu as pltpu
from jax.sharding import PartitionSpec as P

MESH = pl.DeviceIdType.MESH
NX, NY, NZ = 4, 4, 2
TABLE_ROWS = 64
PAD_ROWS = 128
CHUNKS = ((0, 112), (112, 208))
STAGES = 10
F32 = jnp.float32
BF16 = jnp.bfloat16


def chain_part(
    greeted, x_hbm, top_hbm, w_hbm, tab_hbm, ts_ref, dil_ref, gout_ref, part_ref,
    x_ref, w_ref, tab_ref, wt, ht, fw, sp, bt, ups, downs, recv, tacc,
    load_sem, send_sem, recv_sem,
):
    sec = lax.axis_index("section")
    last = lax.axis_size("section") - 1
    core = lax.axis_index("dp") % 2
    groups, bins, chans = x_ref.shape
    steps = tab_ref.shape[0]
    dil = dil_ref[0]

    barrier = pltpu.get_barrier_semaphore()

    @pl.when(sec > 0)
    def _():
        pl.semaphore_signal(barrier, inc=1, device_id={"section": sec - 1}, device_id_type=MESH)

    @pl.when(sec < last)
    def _():
        pl.semaphore_signal(barrier, inc=1, device_id={"section": sec + 1}, device_id_type=MESH)

    table_copy = pltpu.make_async_copy(tab_hbm, tab_ref, load_sem.at[0])
    x_copy = pltpu.make_async_copy(x_hbm, x_ref, load_sem.at[1])
    weight_copy = pltpu.make_async_copy(w_hbm, w_ref, load_sem.at[2])
    top_copy = pltpu.make_async_copy(top_hbm, recv, load_sem.at[3])
    table_copy.start()
    x_copy.start()
    weight_copy.start()

    @pl.when(sec == last)
    def _():
        top_copy.start()

    to_bin = lax.broadcasted_iota(jnp.int32, (bins, bins), 0)
    from_bin = lax.broadcasted_iota(jnp.int32, (bins, bins), 1)
    downs[...] = jnp.where(from_bin == to_bin - dil, 1.0, 0.0).astype(BF16)
    ups[...] = jnp.where(from_bin == to_bin + dil, 1.0, 0.0).astype(BF16)
    step_rows = lax.broadcasted_iota(jnp.int32, (steps, chans), 0)

    def mix(b, carry):
        row = pl.multiple_of(b * bins, bins)
        table = tab_ref[...].astype(F32)
        embed = jnp.sum(jnp.where(step_rows == ts_ref[b], table, 0.0), axis=0, keepdims=True)
        mixed = (x_ref[b].astype(F32) + embed).astype(BF16)
        fw[pl.ds(row, bins), chans : 2 * chans] = mixed
        fw[pl.ds(row, bins), 0:chans] = jnp.dot(
            downs[...], mixed, preferred_element_type=F32
        ).astype(BF16)
        fw[pl.ds(row, bins), 2 * chans :] = jnp.dot(
            ups[...], mixed, preferred_element_type=F32
        ).astype(BF16)
        return carry

    table_copy.wait()
    x_copy.wait()
    lax.fori_loop(0, groups, mix, 0)
    weight_copy.wait()
    for c in range(0, chans, 256):
        preact = jnp.dot(fw[...], w_ref[:, c : c + 256], preferred_element_type=F32)
        gate = jax.nn.sigmoid(preact)
        sp[:, c : c + 256] = gate * (1.0 + preact * (1.0 - gate))
    for tap in range(3):
        wt[tap * chans : (tap + 1) * chans, :] = w_ref[tap * chans : (tap + 1) * chans, :].T
    tacc[...] = jnp.zeros_like(tacc)

    @pl.when(jnp.logical_or(sec < last, core == 1))
    def _():
        ht[...] = fw[:, chans : 2 * chans].T

    @pl.when(jnp.logical_and(sec > 0, sec < last))
    def _():
        pl.semaphore_wait(barrier, greeted + 2)

    @pl.when(jnp.logical_or(sec == 0, sec == last))
    def _():
        pl.semaphore_wait(barrier, greeted + 1)

    @pl.when(sec == last)
    def _():
        top_copy.wait()

    table_rows = lax.broadcasted_iota(jnp.int32, (TABLE_ROWS, chans // 2), 0)

    half = chans // 2

    def hop(b, h):
        span = pl.ds(h * half, half)
        return pltpu.make_async_remote_copy(
            src_ref=gout_ref.at[b, :, span],
            dst_ref=recv.at[b, :, span],
            send_sem=send_sem.at[b, h],
            recv_sem=recv_sem.at[b, h],
            device_id={"section": sec - 1},
            device_id_type=MESH,
        )

    def layer(b, carry):
        rows = pl.ds(pl.multiple_of(b * bins, bins), bins)
        for h in range(2):
            lo, hi = h * half, (h + 1) * half

            @pl.when(sec < last)
            def _():
                hop(b, h).wait_recv()

            delta = (recv[b, :, lo:hi].astype(F32) * sp[rows, lo:hi]).astype(BF16)
            bt[rows, chans + lo : chans + hi] = delta
            bt[rows, lo:hi] = jnp.dot(
                ups[...], delta, preferred_element_type=F32
            ).astype(BF16)
            bt[rows, 2 * chans + lo : 2 * chans + hi] = jnp.dot(
                downs[...], delta, preferred_element_type=F32
            ).astype(BF16)
        for h in range(2):
            lo, hi = h * half, (h + 1) * half
            grad = jnp.dot(bt[rows, :], wt[:, lo:hi], preferred_element_type=F32)
            gout_ref[b, :, lo:hi] = (recv[b, :, lo:hi].astype(F32) + grad).astype(BF16)

            @pl.when(sec > 0)
            def _():
                hop(b, h).start()

            total = jnp.sum(grad, axis=0, keepdims=True)
            tacc[:, lo:hi] += jnp.where(table_rows == ts_ref[b], total, 0.0)
        return carry

    lax.fori_loop(0, groups, layer, 0)

    @pl.when(jnp.logical_and(sec == last, core == 0))
    def _():
        ht[...] = fw[:, chans : 2 * chans].T

    quarter_rows = part_ref.shape[1]

    def put(base, value):
        done = 0
        while done < value.shape[0]:
            q, r = divmod(base + done, quarter_rows)
            size = min(value.shape[0] - done, quarter_rows - r)
            part_ref[q, r : r + size, :] = value[done : done + size, :]
            done += size

    for tap in range(3):
        span = slice(tap * chans, (tap + 1) * chans)
        put(tap * chans, jnp.dot(ht[...], bt[:, span], preferred_element_type=F32).astype(BF16))
    put(3 * chans, tacc[...].astype(BF16))
    put(3 * chans + TABLE_ROWS, jnp.zeros((PAD_ROWS - TABLE_ROWS, chans), BF16))

    @pl.when(sec > 0)
    def _():
        for b in range(groups):
            for h in range(2):
                hop(b, h).wait_send()


def reduce_part(
    scale, run_chain, part_ref, out_ref,
    half_in, half, relay_in, relay, near_in, next_in, quarter, piece_in, piece, far_in,
    send_sem, recv_sem,
):
    dp = lax.axis_index("dp")
    core = dp % 2
    zpos = (dp // 2) % NZ
    ypos = (dp // (2 * NZ)) % NY
    xpos = dp // (2 * NZ * NY)
    side = NX
    width = piece.shape[1]

    def index_of(x, y, z, c):
        return ((x * NY + y) * NZ + z) * 2 + c

    first = xpos * (1 - core) + ypos * core
    second = ypos * (1 - core) + xpos * core

    def at(a, b):
        return index_of(a * (1 - core) + b * core, b * (1 - core) + a * core, zpos, core)

    mate = index_of(xpos, ypos, zpos, 1 - core)
    far = index_of(xpos, ypos, (zpos + 1) % NZ, core)
    ahead, behind = (first + 1) % side, (first + side - 1) % side
    opposite = (first + 2) % side
    peers = [(second + j) % side for j in range(1, side)]
    everyone = [mate, far, at(ahead, second), at(behind, second)] + [at(first, b) for b in peers]

    barrier = pltpu.get_barrier_semaphore()
    for who in everyone:
        pl.semaphore_signal(barrier, inc=1, device_id={"dp": who}, device_id_type=MESH)
    run_chain(len(everyone))

    pending = []

    def send(src, dst, chunk, slot, who):
        copy = pltpu.make_async_remote_copy(
            src_ref=src, dst_ref=dst,
            send_sem=send_sem.at[chunk, slot], recv_sem=recv_sem.at[chunk, slot],
            device_id={"dp": who}, device_id_type=MESH,
        )
        copy.start()
        pending.append(copy)
        return copy

    def cols_at(start, size):
        return pl.ds(pl.multiple_of(start, 128), size)

    mine, theirs = core * side, (1 - core) * side
    own_cols = cols_at(second * width, width)

    def steps(chunk):
        start, stop = CHUNKS[chunk]
        rows = pl.ds(start, stop - start)
        onward, backward = (ahead, behind) if chunk % 2 == 0 else (behind, ahead)

        def forward_to_mate(slot, quarter_id):
            ref = out_ref.at[mine + quarter_id, rows, :]
            return send(ref, ref, chunk, slot, mate)

        copy = send(
            part_ref.at[pl.ds(theirs, side), rows, :], half_in.at[:, rows, :], chunk, 0, mate
        )
        yield
        copy.wait_recv()
        for q in range(side):
            own = part_ref[mine + q, rows, :].astype(F32)
            half[q, rows, :] = (own + half_in[q, rows, :].astype(F32)).astype(BF16)
        passed = send(
            half.at[opposite, rows, :], relay_in.at[rows, :], chunk, 1, at(onward, second)
        )
        direct = send(
            half.at[backward, rows, :], near_in.at[rows, :], chunk, 2, at(backward, second)
        )
        yield
        passed.wait_recv()
        relay[rows, :] = (
            half[onward, rows, :].astype(F32) + relay_in[rows, :].astype(F32)
        ).astype(BF16)
        joined = send(relay.at[rows, :], next_in.at[rows, :], chunk, 3, at(onward, second))
        yield
        direct.wait_recv()
        joined.wait_recv()
        quarter[rows, :] = (
            half[first, rows, :].astype(F32)
            + near_in[rows, :].astype(F32)
            + next_in[rows, :].astype(F32)
        ).astype(BF16)
        copies = [
            send(
                quarter.at[rows, cols_at(b * width, width)], piece_in.at[j, rows, :],
                chunk, 4 + j, at(first, b),
            )
            for j, b in enumerate(peers)
        ]
        yield
        for copy in copies:
            copy.wait_recv()
        total = quarter[rows, own_cols].astype(F32)
        for j in range(side - 1):
            total += piece_in[j, rows, :].astype(F32)
        piece[rows, :] = total.astype(BF16)
        copy = send(piece.at[rows, :], far_in.at[rows, :], chunk, 7, far)
        yield
        copy.wait_recv()
        out_ref[mine + first, rows, own_cols] = (
            (piece[rows, :].astype(F32) + far_in[rows, :].astype(F32)) * scale
        ).astype(BF16)
        block = out_ref.at[mine + first, rows, own_cols]
        copies = [send(block, block, chunk, 8 + j, at(first, b)) for j, b in enumerate(peers)]
        yield
        for copy in copies:
            copy.wait_recv()
        band = out_ref.at[mine + first, rows, :]
        one = send(band, band, chunk, 11, at(onward, second))
        two = send(band, band, chunk, 12, at(backward, second))
        final = [forward_to_mate(14, first)]
        yield
        one.wait_recv()
        band = out_ref.at[mine + backward, rows, :]
        three = send(band, band, chunk, 13, at(onward, second))
        final.append(forward_to_mate(15, backward))
        two.wait_recv()
        final.append(forward_to_mate(16, onward))
        yield
        three.wait_recv()
        final.append(forward_to_mate(17, opposite))
        yield
        for copy in final:
            copy.wait_recv()

    running = [steps(chunk) for chunk in range(len(CHUNKS))]
    for stage in range(STAGES):
        for run in running:
            next(run, None)
    for copy in pending:
        copy.wait_send()


def kernel(scale, *refs):
    operands, (gout_hbm, out_ref), scratch = refs[:6], refs[6:8], refs[8:]
    gout_ref, part_ref, out_sem = scratch[:3]
    chain_scratch, reduce_scratch = scratch[3:18], scratch[18:]
    gout_copy = pltpu.make_async_copy(gout_ref, gout_hbm, out_sem)

    def run_chain(greeted):
        chain_part(greeted, *operands, gout_ref, part_ref, *chain_scratch)
        gout_copy.start()

    reduce_part(scale, run_chain, part_ref, out_ref, *reduce_scratch)
    gout_copy.wait()


def backward(saved, top, weight, table, timesteps, dilations, scale):
    groups, bins, chans = saved.shape
    vmem = pl.BlockSpec(memory_space=pltpu.VMEM)
    hbm = pl.BlockSpec(memory_space=pltpu.HBM)
    smem = pl.BlockSpec(memory_space=pltpu.SMEM)
    taps = 3 * chans
    rows = (taps + PAD_ROWS) // (2 * NX)
    width = chans // NY
    return pl.pallas_call(
        functools.partial(kernel, scale),
        out_shape=(
            jax.ShapeDtypeStruct((groups, bins, chans), BF16),
            jax.ShapeDtypeStruct((2 * NX, rows, chans), BF16),
        ),
        in_specs=[hbm, hbm, hbm, hbm, smem, smem],
        out_specs=(hbm, vmem),
        scratch_shapes=[
            pltpu.VMEM((groups, bins, chans), BF16),
            pltpu.VMEM((2 * NX, rows, chans), BF16),
            pltpu.SemaphoreType.DMA,
            pltpu.VMEM(saved.shape, BF16),
            pltpu.VMEM(weight.shape, BF16),
            pltpu.VMEM(table.shape, BF16),
            pltpu.VMEM((taps, chans), BF16),
            pltpu.VMEM((chans, groups * bins), BF16),
            pltpu.VMEM((groups * bins, taps), BF16),
            pltpu.VMEM((groups * bins, chans), F32),
            pltpu.VMEM((groups * bins, taps), BF16),
            pltpu.VMEM((bins, bins), BF16),
            pltpu.VMEM((bins, bins), BF16),
            pltpu.VMEM((groups, bins, chans), BF16),
            pltpu.VMEM((TABLE_ROWS, chans), F32),
            pltpu.SemaphoreType.DMA((4,)),
            pltpu.SemaphoreType.DMA((groups, 2)),
            pltpu.SemaphoreType.DMA((groups, 2)),
            pltpu.VMEM((NX, rows, chans), BF16),
            pltpu.VMEM((NX, rows, chans), BF16),
            pltpu.VMEM((rows, chans), BF16),
            pltpu.VMEM((rows, chans), BF16),
            pltpu.VMEM((rows, chans), BF16),
            pltpu.VMEM((rows, chans), BF16),
            pltpu.VMEM((rows, chans), BF16),
            pltpu.VMEM((NY - 1, rows, width), BF16),
            pltpu.VMEM((rows, width), BF16),
            pltpu.VMEM((rows, width), BF16),
            pltpu.SemaphoreType.DMA((len(CHUNKS), 18)),
            pltpu.SemaphoreType.DMA((len(CHUNKS), 18)),
        ],
        compiler_params=pltpu.CompilerParams(
            collective_id=0, has_side_effects=True, vmem_limit_bytes=67043328
        ),
        name="backward",
    )(saved, top, weight, table, timesteps, dilations)


def body(section_input, top_grad, conv_weight, step_table, timesteps, dilations):
    taps, chans = conv_weight.shape[1], conv_weight.shape[2]
    groups, bins = top_grad.shape[0], top_grad.shape[1]
    weight = conv_weight.reshape(taps * chans, chans)
    scale = 1.0 / math.sqrt(groups * lax.axis_size("dp") * bins)
    grads, total = backward(
        section_input[0], top_grad, weight, step_table[0], timesteps, dilations, scale
    )
    total = total.reshape(-1, chans)
    weight_out = total[: taps * chans].reshape(1, taps, chans, chans)
    table_out = total[taps * chans : taps * chans + step_table.shape[1]][None]
    return grads[None], weight_out, table_out


def solution(mesh):
    placed = (
        P("section", "dp", None, None),
        P("dp", None, None),
        P("section", None, None, None),
        P("section", None, None),
        P("dp"),
        P("section"),
    )
    return jax.shard_map(
        body,
        mesh=mesh,
        in_specs=placed,
        out_specs=(
            P("section", "dp", None, None),
            P("section", None, None, None),
            P("section", None, None),
        ),
        check_vma=False,
    )
```
